32 devices in a mesh: qrow: 4 (over x, core), kcol: 8 (over z, y).
Axes of the slice: x: 2, y: 2, z: 4, core: 2. Of those that a mesh axis runs over, the one named last changes fastest.
Arguments:
- queries: bfloat16 [4096, 512], P(('qrow', 'kcol')), may hold values from -4.5 to 4.5
- keys: bfloat16 [4096, 128], P(('qrow', 'kcol')), may hold values from -4.5 to 4.5
- values: bfloat16 [4096, 128], P(('qrow', 'kcol')), may hold values from -6 to 6
- upstream: bfloat16 [4096, 512], P(('qrow', 'kcol')), may hold values from -6 to 6
- block_order: int32 [32], replicated, may hold values from 0 to 31, each once
Outputs:
- attended: float32 [4096, 512], P(('qrow', 'kcol'))
- query_grad: float32 [4096, 512], P(('qrow', 'kcol'))
- key_grad: float32 [4096, 128], P(('qrow', 'kcol'))
- value_grad: float32 [4096, 128], P(('qrow', 'kcol'))
The draws below stay inside these ranges and needn't reach their ends.
Inputs may be any that keep to these rules, and one draw needn't show every extreme that they name: `block_order`: each number appears once.
All inputs are finite; a program needn't handle non-finite values.
Results may differ from the reference program's by a relative error of at most 0.0071.
Values may be sent and summed in bfloat16 or wider, within the bound.
No kernel may reach another device: no remote copies, remote signals or barrier semaphores. Data moves between devices by JAX's collectives and lax.ppermute only.
A program may use at most 64 MiB of HBM per device.

```python
import math
import jax
import jax.numpy as jnp
from jax import lax

HEADS = 4
HEAD_DIM = 128
TOK_DEV = 128
BLOCKS = 32
SEQ = 4096


def base_values(key, rows, cols):
    vals = jax.random.normal(jax.random.fold_in(key, 7), (rows, cols), jnp.float32)
    return jnp.clip(vals, -4.5, 4.5)


def draw_keys(key, part):
    vals = base_values(jax.random.fold_in(key, 11), SEQ, HEAD_DIM)
    return vals.astype(jnp.bfloat16)


def draw_queries(key, part):
    vals = base_values(jax.random.fold_in(key, 12), SEQ, HEADS * HEAD_DIM)
    return vals.astype(jnp.bfloat16)


def block_levels(key, dims, shards, smallest, high):
    def one(dim, parts):
        draws = jax.random.uniform(jax.random.fold_in(jax.random.fold_in(key, 6), dim), (parts,), jnp.float32, smallest / len(shards), high / len(shards))
        return jnp.repeat(jnp.exp(draws), dims[dim] // parts).reshape((-1,) + (1,) * (len(dims) - dim - 1))

    level = one(*shards[0])
    for cut in shards[1:]:
        level = level * one(*cut)
    return level


def gaussian(key, dims, scale, most, pieces=(), kind=jnp.bfloat16):
    loudness = block_levels(key, dims, pieces, -0.22, 0.18) if pieces else 1.0
    values = jax.random.normal(key, dims, jnp.float32) * scale * loudness
    return jnp.minimum(jnp.maximum(values, -most), most).astype(kind)


def setup_inputs(seed: int = 0) -> dict:
    key_of = jax.random.split(jax.random.key(seed), 6)
    return {
        "queries": draw_queries(jax.random.fold_in(key_of[5], 71), 0),
        "keys": draw_keys(jax.random.fold_in(key_of[5], 71), 0),
        "values": gaussian(key_of[2], (SEQ, HEAD_DIM), 1.0, 6.0, ((0, 32),)),
        "upstream": gaussian(key_of[3], (SEQ, HEADS * HEAD_DIM), 1.0, 6.0, ((0, 32),)),
        "block_order": jax.random.permutation(key_of[4], BLOCKS).astype(jnp.int32),
    }


def score_block(rows, row_pos, key_rows, key_pos):
    heads = rows.shape[1] // key_rows.shape[1]
    flat = rows.reshape(rows.shape[0] * heads, key_rows.shape[1])
    raw = lax.dot_general(flat, key_rows, (((1,), (1,)), ((), ())), preferred_element_type=jnp.float32)
    raw = raw * (key_rows.shape[1] ** -0.5)
    seen = key_pos[None, :] <= jnp.repeat(row_pos, heads)[:, None]
    return jnp.where(seen, raw, jnp.float32(-1e30))


def block_backward(scores, lse, delta, grad_flat, flat_rows, key_rows, value_rows):
    scale = key_rows.shape[1] ** -0.5
    prob = jnp.exp(scores - lse[:, None])
    weights = prob.astype(jnp.bfloat16)
    value_part = lax.dot_general(weights, grad_flat, (((0,), (0,)), ((), ())), preferred_element_type=jnp.float32)
    dprob = lax.dot_general(grad_flat, value_rows, (((1,), (1,)), ((), ())), preferred_element_type=jnp.float32)
    dscore = (prob * (dprob - delta[:, None])).astype(jnp.bfloat16)
    query_part = jnp.dot(dscore, key_rows, preferred_element_type=jnp.float32) * scale
    key_part = lax.dot_general(dscore, flat_rows, (((0,), (0,)), ((), ())), preferred_element_type=jnp.float32) * scale
    return query_part, key_part, value_part


def reference(queries, keys, values, upstream, block_order):
    offsets = jnp.arange(TOK_DEV, dtype=jnp.int32)
    position = (block_order.astype(jnp.int32)[:, None] * TOK_DEV + offsets[None, :]).reshape(-1)
    width = queries.shape[1]
    step_rows = math.gcd(512, SEQ)
    count = SEQ // step_rows
    head_dim = keys.shape[1]

    def one_block(carry, inputs):
        key_acc, value_acc = carry
        rows, row_pos, grads = inputs
        scores = score_block(rows, row_pos, keys, position)
        top = jnp.max(scores, axis=1)
        total = jnp.sum(jnp.exp(scores - top[:, None]), axis=1)
        lse = top + jnp.log(total)
        weights = jnp.exp(scores - lse[:, None]).astype(jnp.bfloat16)
        out32 = jnp.dot(weights, values, preferred_element_type=jnp.float32)
        grad_flat = grads.reshape(-1, head_dim)
        delta = jnp.sum(grad_flat.astype(jnp.float32) * out32, axis=1)
        flat_rows = rows.reshape(-1, head_dim)
        query_part, key_part, value_part = block_backward(scores, lse, delta, grad_flat, flat_rows, keys, values)
        outs = (out32.reshape(step_rows, width), query_part.reshape(step_rows, width))
        return (key_acc + key_part, value_acc + value_part), outs

    start = (jnp.zeros((SEQ, head_dim), jnp.float32), jnp.zeros((SEQ, head_dim), jnp.float32))
    inputs = (queries.reshape(count, step_rows, width), position.reshape(count, step_rows), upstream.reshape(count, step_rows, width))
    (key_acc, value_acc), (attended, query_grad) = lax.scan(one_block, start, inputs)
    return (attended.reshape(SEQ, width), query_grad.reshape(SEQ, width), key_acc, value_acc)
```

```python
import math

import jax
import jax.numpy as jnp
from jax import lax
from jax.experimental import pallas as pl
from jax.experimental.pallas import tpu as pltpu
from jax.sharding import PartitionSpec as P

AXES = ("qrow", "kcol")
F32, BF16 = jnp.float32, jnp.bfloat16
HIDDEN = 1e30
FLOOR = -1e29
LOG2E = math.log2(math.e)
VMEM = pl.BlockSpec(memory_space=pltpu.VMEM)
SMEM = pl.BlockSpec(memory_space=pltpu.SMEM)


def spread(bits):
    return [
        sum(bit for place, bit in enumerate(bits) if index >> place & 1)
        for index in range(1 << len(bits))
    ]


def swap(value, mask, devices):
    return lax.ppermute(value, AXES, [(i, i ^ mask) for i in range(devices)])


def nt(a, b):
    return lax.dot_general(a, b, (((1,), (1,)), ((), ())), preferred_element_type=F32)


def nn(a, b):
    return lax.dot_general(a, b, (((1,), (0,)), ((), ())), preferred_element_type=F32)


def tn(a, b):
    return lax.dot_general(a, b, (((0,), (0,)), ((), ())), preferred_element_type=F32)


def by_head(ref, dim):
    return jnp.concatenate(
        [ref[:, at : at + dim] for at in range(0, ref.shape[1], dim)], axis=0
    )


def seen_in_block(tok, rows):
    key = lax.broadcasted_iota(jnp.int32, (tok, rows), 0)
    row = lax.broadcasted_iota(jnp.int32, (tok, rows), 1) % tok
    return key <= row


def bias_of(order_ref, row_block, key_block):
    seen = order_ref[key_block] <= order_ref[row_block]
    return jnp.where(seen, jnp.float32(0.0), jnp.float32(HIDDEN))


def forward_kernel(row_masks, key_masks, me_ref, order_ref, *refs):
    nr, nk = len(row_masks), len(key_masks)
    qs, ds, kvs = refs[:nr], refs[nr : 2 * nr], refs[2 * nr : 2 * nr + nk]
    stats_ref, *outs = refs[2 * nr + nk : -1]
    s_ref = refs[-1]
    tok, width = qs[0].shape
    dim = kvs[0].shape[1] // 2
    rows = tok * (width // dim)
    unit = dim**-0.5 * LOG2E
    me = me_ref[0]
    for r in range(nr):
        q = by_head(qs[r], dim)
        top = None
        for j in range(nk):
            s = nt(kvs[j][:, :dim], q) * unit
            if r == 0 and j == 0:
                s = jnp.where(seen_in_block(tok, rows), s, -HIDDEN)
                bias = jnp.float32(0.0)
            else:
                bias = bias_of(order_ref, me ^ row_masks[r], me ^ key_masks[j])
            s_ref[j * tok : (j + 1) * tok, :] = s
            part = jnp.max(s, axis=0, keepdims=True) - bias
            top = part if top is None else jnp.maximum(top, part)
        top = jnp.maximum(top, FLOOR)
        total, acc = None, None
        for j in range(nk):
            if r == 0 and j == 0:
                bias = jnp.float32(0.0)
            else:
                bias = bias_of(order_ref, me ^ row_masks[r], me ^ key_masks[j])
            p = jnp.exp2(s_ref[j * tok : (j + 1) * tok, :] - (top + bias))
            part = jnp.sum(p, axis=0, keepdims=True)
            total = part if total is None else total + part
            out = tn(kvs[j][:, dim:], p.astype(BF16))
            acc = out if acc is None else acc + out
        prods = []
        for h in range(width // dim):
            span = slice(h * tok, (h + 1) * tok)
            piece = acc[:, span]
            grads = ds[r][:, h * dim : (h + 1) * dim].astype(F32).T
            prods.append(jnp.sum(piece * grads, axis=0, keepdims=True))
            outs[r][:, h * dim : (h + 1) * dim] = piece.T.astype(outs[r].dtype)
        stats_ref[4 * r : 4 * r + 1, :] = top
        stats_ref[4 * r + 1 : 4 * r + 2, :] = total
        stats_ref[4 * r + 2 : 4 * r + 3, :] = jnp.concatenate(prods, axis=1)
        stats_ref[4 * r + 3 : 4 * r + 4, :] = jnp.zeros_like(top)


def joined(stats, r):
    tops = [ref[4 * (r ^ a) : 4 * (r ^ a) + 1, :] for a, ref in enumerate(stats)]
    best = tops[0]
    for top in tops[1:]:
        best = jnp.maximum(best, top)
    shares = [jnp.exp2(top - best) for top in tops]
    total = sum(
        share * ref[4 * (r ^ a) + 1 : 4 * (r ^ a) + 2, :]
        for a, (share, ref) in enumerate(zip(shares, stats))
    )
    prods = sum(
        share * ref[4 * (r ^ a) + 2 : 4 * (r ^ a) + 3, :]
        for a, (share, ref) in enumerate(zip(shares, stats))
    )
    inverse = 1.0 / total
    return [share * inverse for share in shares], best + jnp.log2(total), prods * inverse


def backward_kernel(row_masks, key_masks, me_ref, order_ref, *refs):
    nr, nk = len(row_masks), len(key_masks)
    stats = refs[:nr]
    qs, ds, kvs = refs[nr : 2 * nr], refs[2 * nr : 3 * nr], refs[3 * nr : 3 * nr + nk]
    outs = refs[3 * nr + nk : 4 * nr + nk]
    keep_ref, send_ref, acc_ref = refs[4 * nr + nk :]
    tok, width = qs[0].shape
    dim = kvs[0].shape[1] // 2
    rows = tok * (width // dim)
    scale = dim**-0.5
    me = me_ref[0]
    for r in range(nr):
        q, d = by_head(qs[r], dim), by_head(ds[r], dim)
        _, lse, delta = joined(stats, r)
        acc = None
        for j in range(nk):
            k, v = kvs[j][:, :dim], kvs[j][:, dim:]
            s = nt(k, q) * (scale * LOG2E)
            if r == 0 and j == 0:
                p = jnp.where(seen_in_block(tok, rows), jnp.exp2(s - lse), 0.0)
            else:
                p = jnp.exp2(s - (lse + bias_of(order_ref, me ^ row_masks[r], me ^ key_masks[j])))
            t = (p * (nt(v, d) - delta)).astype(BF16)
            span = slice(j * tok, (j + 1) * tok)
            key_part, value_part = nn(t, q), nn(p.astype(BF16), d)
            if r == 0:
                acc_ref[span, :dim] = key_part
                acc_ref[span, dim:] = value_part
            else:
                acc_ref[span, :dim] += key_part
                acc_ref[span, dim:] += value_part
            out = tn(k, t)
            acc = out if acc is None else acc + out
        for h in range(width // dim):
            piece = acc[:, h * tok : (h + 1) * tok].T * scale
            outs[r][:, h * dim : (h + 1) * dim] = piece.astype(outs[r].dtype)
    half = keep_ref.shape[0]
    for ref, at in ((keep_ref, 0), (send_ref, half)):
        ref[:, :dim] = (acc_ref[at : at + half, :dim] * scale).astype(ref.dtype)
        ref[:, dim:] = acc_ref[at : at + half, dim:].astype(ref.dtype)


def pair_kernel(keep_ref, got_ref, own_ref, *sends):
    tok = own_ref.shape[0]
    for i, ref in enumerate((own_ref, *sends)):
        span = slice(i * tok, (i + 1) * tok)
        ref[...] = (keep_ref[span, :] + got_ref[span, :].astype(F32)).astype(ref.dtype)


def sum_kernel(*refs):
    *ins, out = refs
    total = ins[0][...]
    for ref in ins[1:]:
        total += ref[...].astype(F32)
    out[...] = total


def key_sum_kernel(*refs):
    *ins, key_ref, value_ref = refs
    dim = key_ref.shape[1]
    total = ins[0][...]
    for ref in ins[1:]:
        total += ref[...].astype(F32)
    key_ref[...] = total[:, :dim]
    value_ref[...] = total[:, dim:]


def attended_kernel(count, dim, *refs):
    stats, parts, out = refs[:count], refs[count : 2 * count], refs[2 * count]
    tok, width = out.shape
    shares, _, _ = joined(stats, 0)
    for h in range(width // dim):
        total = None
        for a in range(count):
            row = shares[a][:, h * tok : (h + 1) * tok]
            column = jnp.broadcast_to(row, (tok, tok)).T[:, :1]
            part = parts[a][:, h * dim : (h + 1) * dim].astype(F32) * column
            total = part if total is None else total + part
        out[:, h * dim : (h + 1) * dim] = total


def call(kernel, outs, *args, scalars=0, scratch=(), flops=0):
    nbytes = sum(a.size * a.dtype.itemsize for a in (*args, *outs))
    return pl.pallas_call(
        kernel,
        out_shape=outs,
        in_specs=[SMEM] * scalars + [VMEM] * (len(args) - scalars),
        out_specs=[VMEM] * len(outs),
        scratch_shapes=list(scratch),
        cost_estimate=pl.CostEstimate(flops=flops, bytes_accessed=nbytes, transcendentals=0),
    )(*args)


def per_device(queries, keys, values, upstream, block_order):
    tok, width = queries.shape
    dim = keys.shape[1]
    heads = width // dim
    rows = tok * heads
    nrow, ncol = lax.axis_size("qrow"), lax.axis_size("kcol")
    devices = nrow * ncol
    row_bits = [ncol << i for i in range(1, nrow.bit_length() - 1)] + [1]
    far_bits = [1 << i for i in range(1, ncol.bit_length() - 1)]
    pair = ncol
    row_masks = spread(row_bits)
    far_masks = spread(far_bits)
    key_masks = far_masks + [pair | mask for mask in far_masks]
    nr, nf, nk = len(row_masks), len(far_masks), len(key_masks)
    me = (lax.axis_index("qrow") * ncol + lax.axis_index("kcol")).astype(jnp.int32).reshape(1)

    def send(value, mask):
        return swap(value, mask, devices)

    def shape(dims, kind):
        return jax.ShapeDtypeStruct(dims, kind)

    def relayed(value, bits):
        parts = {0: value}
        for bit in bits:
            parts.update({mask | bit: send(part, bit) for mask, part in list(parts.items())})
        return [parts[mask] for mask in row_masks]

    q = relayed(queries, row_bits)
    d = relayed(upstream, row_bits[::-1])
    own = jnp.concatenate([keys, values], axis=1)
    far = [own] + [send(own, mask) for mask in far_masks[1:]]
    kv = far + [send(part, pair) for part in far]

    work = 2 * rows * nr * tok * nk * dim
    stats, *parts = call(
        lambda *refs: forward_kernel(row_masks, key_masks, *refs),
        [shape((4 * nr, rows), F32), shape((tok, width), F32)]
        + [shape((tok, width), BF16)] * (nr - 1),
        me, block_order, *q, *d, *kv,
        scalars=2, scratch=[pltpu.VMEM((nk * tok, rows), F32)], flops=2 * work,
    )
    all_stats = [stats] + [send(stats, mask) for mask in row_masks[1:]]
    all_parts = parts[:1] + [send(p, mask) for p, mask in zip(parts[1:], row_masks[1:])]
    *query_parts, keep, give = call(
        lambda *refs: backward_kernel(row_masks, key_masks, *refs),
        [shape((tok, width), F32)]
        + [shape((tok, width), BF16)] * (nr - 1)
        + [shape((nf * tok, 2 * dim), F32), shape((nf * tok, 2 * dim), BF16)],
        me, block_order, *all_stats, *q, *d, *kv,
        scalars=2, scratch=[pltpu.VMEM((nk * tok, 2 * dim), F32)], flops=5 * work,
    )
    got = send(give, pair)
    own_kv, *far_kv = call(
        pair_kernel,
        [shape((tok, 2 * dim), F32)] + [shape((tok, 2 * dim), BF16)] * (nf - 1),
        keep, got,
    )
    query_in = [send(p, mask) for p, mask in zip(query_parts[1:], row_masks[1:])]
    far_in = [send(p, mask) for p, mask in zip(far_kv, far_masks[1:])]
    (attended,) = call(
        lambda *refs: attended_kernel(nr, dim, *refs),
        [shape((tok, width), F32)], *all_stats, *all_parts,
    )
    (query_grad,) = call(sum_kernel, [shape((tok, width), F32)], query_parts[0], *query_in)
    key_grad, value_grad = call(key_sum_kernel, [shape((tok, dim), F32)] * 2, own_kv, *far_in)
    return attended, query_grad, key_grad, value_grad


def solution(mesh):
    spec = P(AXES, None)
    return jax.shard_map(
        per_device,
        mesh=mesh,
        in_specs=(spec,) * 4 + (P(),),
        out_specs=(spec,) * 4,
        check_vma=False,
    )
```

```python
import math

import jax
import jax.numpy as jnp
from jax import lax
from jax.experimental import pallas as pl
from jax.experimental.pallas import tpu as pltpu
from jax.sharding import PartitionSpec as P


AXES = ("qrow", "kcol")
F32, BF16 = jnp.float32, jnp.bfloat16
HIDDEN = 1e30
FLOOR = -1e29
LOG2E = math.log2(math.e)
VMEM = pl.BlockSpec(memory_space=pltpu.VMEM)
SMEM = pl.BlockSpec(memory_space=pltpu.SMEM)


def spread(bits):
    return [
        sum(bit for place, bit in enumerate(bits) if index >> place & 1)
        for index in range(1 << len(bits))
    ]


def swap(value, mask, devices):
    return lax.ppermute(value, AXES, [(i, i ^ mask) for i in range(devices)])


def nt(a, b):
    return lax.dot_general(a, b, (((1,), (1,)), ((), ())), preferred_element_type=F32)


def nn(a, b):
    return lax.dot_general(a, b, (((1,), (0,)), ((), ())), preferred_element_type=F32)


def tn(a, b):
    return lax.dot_general(a, b, (((0,), (0,)), ((), ())), preferred_element_type=F32)


def by_head(ref, dim, start, width):
    return jnp.concatenate(
        [ref[:, at : at + dim].T for at in range(start, start + width, dim)], axis=1
    )


def pieces(value, count):
    parts = []
    for _ in range(count):
        part = value.astype(BF16)
        value = value - part.astype(F32)
        parts.append(part)
    return parts


def seen_in_block(tok, rows):
    key = lax.broadcasted_iota(jnp.int32, (tok, rows), 0)
    row = lax.broadcasted_iota(jnp.int32, (tok, rows), 1) % tok
    return key <= row


def pack_kernel(row_masks, key_masks, me_ref, table_ref, *refs):
    ins, (rows_ref, keys_ref, bias_ref, order_ref, sems) = refs[:4], refs[4:]
    width, dim = ins[0].shape[1], ins[2].shape[1]
    spots = [
        rows_ref.at[:, :width],
        rows_ref.at[:, width:],
        keys_ref.at[:, :dim],
        keys_ref.at[:, dim:],
    ]
    copies = [
        pltpu.make_async_copy(source, spot, sems.at[i])
        for i, (source, spot) in enumerate(zip((table_ref, *ins), (order_ref, *spots)))
    ]
    for copy in copies:
        copy.start()
    copies[0].wait()
    me = me_ref[0]
    lane = lax.broadcasted_iota(jnp.int32, (1, bias_ref.shape[1]), 1)
    for r, row_mask in enumerate(row_masks):
        row = jnp.zeros(lane.shape, F32)
        for j, key_mask in enumerate(key_masks):
            seen = order_ref[me ^ key_mask] <= order_ref[me ^ row_mask]
            row = jnp.where(lane == j, jnp.where(seen, jnp.float32(0.0), jnp.float32(HIDDEN)), row)
        bias_ref[r : r + 1, :] = row
    for copy in copies[1:]:
        copy.wait()


def forward_kernel(nr, nk, bias_ref, *refs):
    qds, kvs = refs[:nr], refs[nr : nr + nk]
    stats_ref, p_ref, qt_ref, dt_ref = refs[nr + nk : nr + nk + 4]
    outs, (kk_ref, v_ref, s_ref) = refs[nr + nk + 4 : -3], refs[-3:]
    tok, width = qds[0].shape[0], qds[0].shape[1] // 2
    dim = kvs[0].shape[1] // 2
    rows = tok * (width // dim)
    unit = dim**-0.5 * LOG2E
    for j, ref in enumerate(kvs):
        span = slice(j * tok, (j + 1) * tok)
        kk_ref[span, :dim] = ref[:, :dim]
        kk_ref[span, dim:] = ref[:, :dim]
        v_ref[span, :] = ref[:, dim:]

    def score(r):
        q = by_head(qds[r], dim, 0, width)
        qt_ref[:, r * rows : (r + 1) * rows] = q
        scaled = jnp.concatenate(pieces(q.astype(F32) * unit, 2), axis=0)
        s_ref[r % 2] = nn(kk_ref[...], scaled)

    score(0)
    for r in range(nr):
        slot, lanes = r % 2, slice(r * rows, (r + 1) * rows)
        biases, top = [], None
        for j in range(nk):
            span = slice(j * tok, (j + 1) * tok)
            s = s_ref[slot, span, :]
            if r == 0 and j == 0:
                s = jnp.where(seen_in_block(tok, rows), s, -HIDDEN)
                s_ref[slot, span, :] = s
            bias = bias_ref[r : r + 1, j : j + 1]
            biases.append(bias)
            part = jnp.max(s, axis=0, keepdims=True) - bias
            top = part if top is None else jnp.maximum(top, part)
        top = jnp.maximum(top, FLOOR)
        if r + 1 < nr:
            score(r + 1)
        total = None
        for j in range(nk):
            span = slice(j * tok, (j + 1) * tok)
            p = jnp.exp2(s_ref[slot, span, :] - (top + biases[j]))
            part = jnp.sum(p, axis=0, keepdims=True)
            total = part if total is None else total + part
            p_ref[span, lanes] = p.astype(BF16)
        d = by_head(qds[r], dim, width, width)
        dt_ref[:, lanes] = d
        out = tn(v_ref[...], p_ref[:, lanes])
        for h in range(width // dim):
            piece = out[:, h * tok : (h + 1) * tok].astype(outs[r].dtype).T
            outs[r][:, h * dim : (h + 1) * dim] = piece
        stats_ref[4 * r : 4 * r + 1, :] = top
        stats_ref[4 * r + 1 : 4 * r + 2, :] = total
        stats_ref[4 * r + 2 : 4 * r + 3, :] = jnp.sum(out * d.astype(F32), axis=0, keepdims=True)
        stats_ref[4 * r + 3 : 4 * r + 4, :] = jnp.zeros_like(top)


def joined(stats, r):
    held = [ref[4 * (r ^ a) : 4 * (r ^ a) + 3, :] for a, ref in enumerate(stats)]
    best = held[0][0:1]
    for part in held[1:]:
        best = jnp.maximum(best, part[0:1])
    shares = [jnp.exp2(part[0:1] - best) for part in held]
    total = sum(share * part[1:2] for share, part in zip(shares, held))
    prods = sum(share * part[2:3] for share, part in zip(shares, held))
    inverse = 1.0 / total
    return [share * inverse for share in shares], prods * inverse


def backward_kernel(nr, nk, *refs):
    p_ref, qt_ref, dt_ref = refs[:3]
    stats, kvs = refs[3 : nr + 3], refs[nr + 3 : nr + nk + 3]
    outs = refs[nr + nk + 3 : 2 * nr + nk + 3]
    keep_ref, send_ref, k_ref, v_ref, da_ref, g_ref, t_ref, acc_ref = refs[2 * nr + nk + 3 :]
    tok, dim = kvs[0].shape[0], kvs[0].shape[1] // 2
    rows = p_ref.shape[1] // nr
    width = rows // tok * dim
    scale = dim**-0.5
    lane = lax.broadcasted_iota(jnp.int32, (tok, dim), 1)
    ones = jnp.where(lane < 3, jnp.float32(1.0), jnp.float32(0.0)).astype(BF16)
    for j, ref in enumerate(kvs):
        span = slice(j * tok, (j + 1) * tok)
        k_ref[span, :] = ref[:, :dim]
        v_ref[span, :dim] = ref[:, dim:]
        v_ref[span, dim:] = ones
    fill = jnp.zeros((dim - 3, rows), BF16)

    def grads(r):
        slot, lanes = r % 2, slice(r * rows, (r + 1) * rows)
        (share, *_), delta = joined(stats, r)
        da_ref[slot, :dim, :] = dt_ref[:, lanes]
        da_ref[slot, dim:, :] = jnp.concatenate(pieces(-delta, 3) + [fill], axis=0)
        g_ref[slot] = nn(v_ref[...], da_ref[slot])
        return share

    share = grads(0)
    for r in range(nr):
        slot, lanes = r % 2, slice(r * rows, (r + 1) * rows)
        after = grads(r + 1) if r + 1 < nr else None
        for j in range(nk):
            span = slice(j * tok, (j + 1) * tok)
            p = p_ref[span, lanes].astype(F32)
            t_ref[slot, span, :] = (p * g_ref[slot, span, :]).astype(BF16)
        value_part = nt((dt_ref[:, lanes].astype(F32) * share).astype(BF16), p_ref[:, lanes])
        key_part = nt((qt_ref[:, lanes].astype(F32) * share).astype(BF16), t_ref[slot])
        if r == 0:
            acc_ref[:dim, :] = key_part
            acc_ref[dim:, :] = value_part
        else:
            acc_ref[:dim, :] += key_part
            acc_ref[dim:, :] += value_part
        query_part = tn(k_ref[...], t_ref[slot]) * (share * scale)
        for h in range(width // dim):
            piece = query_part[:, h * tok : (h + 1) * tok].astype(outs[r].dtype).T
            outs[r][:, h * dim : (h + 1) * dim] = piece
        share = after
    half = nk // 2
    for j in range(nk):
        ref = keep_ref if j < half else send_ref
        span = slice(j % half * tok, (j % half + 1) * tok)
        cols = slice(j * tok, (j + 1) * tok)
        ref[span, :dim] = (acc_ref[:dim, cols] * scale).astype(ref.dtype).T
        ref[span, dim:] = acc_ref[dim:, cols].astype(ref.dtype).T


def attended_kernel(count, dim, *refs):
    stats, parts, out = refs[:count], refs[count : 2 * count], refs[2 * count]
    tok, width = out.shape
    shares, _ = joined(stats, 0)
    for h in range(width // dim):
        total = None
        across = [share[:, h * tok : (h + 1) * tok] for share in shares]
        across += [jnp.zeros_like(across[0])] * (-count % 8)
        columns = jnp.concatenate(across, axis=0).T
        for a in range(count):
            part = parts[a][:, h * dim : (h + 1) * dim].astype(F32) * columns[:, a : a + 1]
            total = part if total is None else total + part
        out[:, h * dim : (h + 1) * dim] = total


def call(kernel, outs, *args, scalars=0, spaces=VMEM, scratch=(), flops=0, room=None):
    nbytes = sum(a.size * a.dtype.itemsize for a in (*args, *outs))
    return pl.pallas_call(
        kernel,
        out_shape=outs,
        in_specs=[SMEM] * scalars + [spaces] * (len(args) - scalars),
        out_specs=[VMEM] * len(outs),
        scratch_shapes=list(scratch),
        compiler_params=pltpu.CompilerParams(vmem_limit_bytes=room) if room else None,
        cost_estimate=pl.CostEstimate(flops=flops, bytes_accessed=nbytes, transcendentals=0),
    )(*args)


def per_device(queries, keys, values, upstream, block_order):
    tok, width = queries.shape
    dim = keys.shape[1]
    heads = width // dim
    rows = tok * heads
    nrow, ncol = lax.axis_size("qrow"), lax.axis_size("kcol")
    devices = nrow * ncol
    row_bits = [ncol << i for i in range(1, nrow.bit_length() - 1)] + [1]
    far_bits = [1 << i for i in range(1, ncol.bit_length() - 1)]
    pair = ncol
    row_masks = spread(row_bits)
    far_masks = spread(far_bits)
    key_masks = far_masks + [pair | mask for mask in far_masks]
    nr, nf, nk = len(row_masks), len(far_masks), len(key_masks)
    me = (lax.axis_index("qrow") * ncol + lax.axis_index("kcol")).astype(jnp.int32).reshape(1)

    def send(value, mask):
        return swap(value, mask, devices)

    def spray(values, masks):
        return [send(v, mask) for v, mask in zip(values, masks[1:])]

    def shape(dims, kind):
        return jax.ShapeDtypeStruct(dims, kind)

    given = (block_order, queries, upstream, keys, values)
    own_rows, own, bias = call(
        lambda *refs: pack_kernel(row_masks, key_masks, *refs),
        [
            shape((tok, 2 * width), BF16),
            shape((tok, 2 * dim), BF16),
            shape((nr, max(128, nk)), F32),
        ],
        me, *[pltpu.with_memory_space_constraint(a, pltpu.HBM) for a in given],
        scalars=1, spaces=pl.BlockSpec(memory_space=pltpu.HBM),
        scratch=[pltpu.SMEM(block_order.shape, jnp.int32), pltpu.SemaphoreType.DMA((5,))],
        room=4 << 20,
    )
    qd = [own_rows] + spray([own_rows] * (nr - 1), row_masks)
    far = [own] + spray([own] * (nf - 1), far_masks)
    kv = far + [send(part, pair) for part in far]

    score = pltpu.VMEM((2, nk * tok, rows), F32)
    narrow, wide = pltpu.VMEM((nk * tok, dim), BF16), pltpu.VMEM((nk * tok, 2 * dim), BF16)
    room = 4 * nk * tok * nr * rows
    work = 2 * rows * nr * tok * nk * dim
    stats, weights, flat_q, flat_d, *parts = call(
        lambda *refs: forward_kernel(nr, nk, *refs),
        [
            shape((4 * nr, rows), F32),
            shape((nk * tok, nr * rows), BF16),
            shape((dim, nr * rows), BF16),
            shape((dim, nr * rows), BF16),
            shape((tok, width), F32),
        ]
        + [shape((tok, width), BF16)] * (nr - 1),
        bias, *qd, *kv,
        scratch=[wide, narrow, score], flops=2 * work, room=room + (6 << 20),
    )
    all_stats = [stats] + spray([stats] * (nr - 1), row_masks)
    all_parts = parts[:1] + spray(parts[1:], row_masks)
    *row_parts, keep, give = call(
        lambda *refs: backward_kernel(nr, nk, *refs),
        [shape((tok, width), F32)]
        + [shape((tok, width), BF16)] * (nr - 1)
        + [shape((nf * tok, 2 * dim), F32), shape((nf * tok, 2 * dim), BF16)],
        weights, flat_q, flat_d, *all_stats, *kv,
        scratch=[
            narrow,
            wide,
            pltpu.VMEM((2, 2 * dim, rows), BF16),
            score,
            pltpu.VMEM((2, nk * tok, rows), BF16),
            pltpu.VMEM((2 * dim, nk * tok), F32),
        ],
        flops=4 * work,
        room=room + (8 << 20),
    )
    got = send(give, pair)
    summed = keep + got.astype(F32)
    own_kv, *far_kv = [summed[i * tok : (i + 1) * tok] for i in range(nf)]
    far_kv = [part.astype(BF16) for part in far_kv]
    rows_in = spray(row_parts[1:], row_masks)
    far_in = spray(far_kv, far_masks)
    (attended,) = call(
        lambda *refs: attended_kernel(nr, dim, *refs),
        [shape((tok, width), F32)], *all_stats, *all_parts,
        room=8 * nr * tok * width + (4 << 20),
    )
    query_grad = row_parts[0] + sum(part.astype(F32) for part in rows_in)
    key_sum = own_kv + sum(part.astype(F32) for part in far_in)
    key_grad, value_grad = key_sum[:, :dim], key_sum[:, dim:]
    return attended, query_grad, key_grad, value_grad


def solution(mesh):
    spec = P(AXES, None)

    return jax.shard_map(
        per_device,
        mesh=mesh,
        in_specs=(spec,) * 4 + (P(),),
        out_specs=(spec,) * 4,
        check_vma=False,
    )
```

```python
import math

import jax
import jax.numpy as jnp
from jax import lax
from jax.experimental import pallas as pl
from jax.experimental.pallas import tpu as pltpu
from jax.sharding import PartitionSpec as P


AXES = ("qrow", "kcol")
F32, BF16 = jnp.float32, jnp.bfloat16
HIDDEN = 1e30
FLOOR = -1e29
LOG2E = math.log2(math.e)
VMEM = pl.BlockSpec(memory_space=pltpu.VMEM)
SMEM = pl.BlockSpec(memory_space=pltpu.SMEM)


def spread(bits):
    return [
        sum(bit for place, bit in enumerate(bits) if index >> place & 1)
        for index in range(1 << len(bits))
    ]


def swap(value, mask, devices):
    return lax.ppermute(value, AXES, [(i, i ^ mask) for i in range(devices)])


def nn(a, b):
    return lax.dot_general(a, b, (((1,), (0,)), ((), ())), preferred_element_type=F32)


def tn(a, b):
    return lax.dot_general(a, b, (((0,), (0,)), ((), ())), preferred_element_type=F32)


def by_head(ref, dim, start, width):
    return jnp.concatenate(
        [ref[:, at : at + dim].T for at in range(start, start + width, dim)], axis=1
    )


def pieces(value, count):
    parts = []
    for _ in range(count):
        part = value.astype(BF16)
        value = value - part.astype(F32)
        parts.append(part)
    return parts


def seen_in_block(tok, rows):
    key = lax.broadcasted_iota(jnp.int32, (tok, rows), 0)
    row = lax.broadcasted_iota(jnp.int32, (tok, rows), 1) % tok
    return key <= row


def pack_kernel(row_masks, key_masks, me_ref, table_ref, *refs):
    ins, (rows_ref, keys_ref, bias_ref, order_ref, sems) = refs[:4], refs[4:]
    width, dim = ins[0].shape[1], ins[2].shape[1]
    spots = [
        rows_ref.at[:, :width],
        rows_ref.at[:, width:],
        keys_ref.at[:, :dim],
        keys_ref.at[:, dim:],
    ]
    copies = [
        pltpu.make_async_copy(source, spot, sems.at[i])
        for i, (source, spot) in enumerate(zip((table_ref, *ins), (order_ref, *spots)))
    ]
    for copy in copies:
        copy.start()
    copies[0].wait()
    me = me_ref[0]
    lane = lax.broadcasted_iota(jnp.int32, (1, bias_ref.shape[1]), 1)
    for r, row_mask in enumerate(row_masks):
        row = jnp.zeros(lane.shape, F32)
        for j, key_mask in enumerate(key_masks):
            seen = order_ref[me ^ key_mask] <= order_ref[me ^ row_mask]
            row = jnp.where(lane == j, jnp.where(seen, jnp.float32(0.0), jnp.float32(HIDDEN)), row)
        bias_ref[r : r + 1, :] = row
    for copy in copies[1:]:
        copy.wait()


def forward_kernel(nr, nk, bias_ref, *refs):
    qds, kvs = refs[:nr], refs[nr : nr + nk]
    stats_ref, p_ref, qt_ref, dt_ref = refs[nr + nk : nr + nk + 4]
    outs, (kk_ref, v_ref, s_ref) = refs[nr + nk + 4 : -3], refs[-3:]
    tok, width = qds[0].shape[0], qds[0].shape[1] // 2
    dim = kvs[0].shape[1] // 2
    rows = tok * (width // dim)
    unit = dim**-0.5 * LOG2E
    for j, ref in enumerate(kvs):
        span = slice(j * tok, (j + 1) * tok)
        kk_ref[span, :dim] = ref[:, :dim]
        kk_ref[span, dim:] = ref[:, :dim]
        v_ref[span, :] = ref[:, dim:]

    def score(r):
        q = by_head(qds[r], dim, 0, width)
        qt_ref[:, r * rows : (r + 1) * rows] = q
        scaled = jnp.concatenate(pieces(q.astype(F32) * unit, 2), axis=0)
        s_ref[r % 2] = nn(kk_ref[...], scaled)

    score(0)
    for r in range(nr):
        slot, lanes = r % 2, slice(r * rows, (r + 1) * rows)
        biases, top = [], None
        for j in range(nk):
            span = slice(j * tok, (j + 1) * tok)
            s = s_ref[slot, span, :]
            if r == 0 and j == 0:
                s = jnp.where(seen_in_block(tok, rows), s, -HIDDEN)
                s_ref[slot, span, :] = s
            bias = bias_ref[r : r + 1, j : j + 1]
            biases.append(bias)
            part = jnp.max(s, axis=0, keepdims=True) - bias
            top = part if top is None else jnp.maximum(top, part)
        top = jnp.maximum(top, FLOOR)
        if r + 1 < nr:
            score(r + 1)
        total = None
        for j in range(nk):
            span = slice(j * tok, (j + 1) * tok)
            p = jnp.exp2(s_ref[slot, span, :] - (top + biases[j]))
            part = jnp.sum(p, axis=0, keepdims=True)
            total = part if total is None else total + part
            p_ref[span, lanes] = p.astype(BF16)
        d = by_head(qds[r], dim, width, width)
        dt_ref[:, lanes] = d
        out = tn(v_ref[...], p_ref[:, lanes])
        for h in range(width // dim):
            piece = out[:, h * tok : (h + 1) * tok].astype(outs[r].dtype).T
            outs[r][:, h * dim : (h + 1) * dim] = piece
        stats_ref[4 * r : 4 * r + 1, :] = top
        stats_ref[4 * r + 1 : 4 * r + 2, :] = total
        stats_ref[4 * r + 2 : 4 * r + 3, :] = jnp.sum(out * d.astype(F32), axis=0, keepdims=True)
        stats_ref[4 * r + 3 : 4 * r + 4, :] = jnp.zeros_like(top)


def joined(stats, r):
    held = [ref[4 * (r ^ a) : 4 * (r ^ a) + 3, :] for a, ref in enumerate(stats)]
    best = held[0][0:1]
    for part in held[1:]:
        best = jnp.maximum(best, part[0:1])
    shares = [jnp.exp2(part[0:1] - best) for part in held]
    total = sum(share * part[1:2] for share, part in zip(shares, held))
    prods = sum(share * part[2:3] for share, part in zip(shares, held))
    inverse = 1.0 / total
    return [share * inverse for share in shares], prods * inverse


def backward_kernel(nr, nk, *refs):
    p_ref, qt_ref, dt_ref = refs[:3]
    stats, kvs = refs[3 : nr + 3], refs[nr + 3 : nr + nk + 3]
    outs = refs[nr + nk + 3 : 2 * nr + nk + 3]
    keep_ref, send_ref, k_ref, v_ref, da_ref, g_ref, t_ref, acc_ref = refs[2 * nr + nk + 3 :]
    tok, dim = kvs[0].shape[0], kvs[0].shape[1] // 2
    rows = p_ref.shape[1] // nr
    width = rows // tok * dim
    scale = dim**-0.5
    lane = lax.broadcasted_iota(jnp.int32, (tok, dim), 1)
    ones = jnp.where(lane < 3, jnp.float32(1.0), jnp.float32(0.0)).astype(BF16)
    for j, ref in enumerate(kvs):
        span = slice(j * tok, (j + 1) * tok)
        k_ref[span, :] = ref[:, :dim]
        v_ref[span, :dim] = ref[:, dim:]
        v_ref[span, dim:] = ones
    fill = jnp.zeros((dim - 3, rows), BF16)

    def grads(r):
        slot, lanes = r % 2, slice(r * rows, (r + 1) * rows)
        (share, *_), delta = joined(stats, r)
        da_ref[slot, :dim, :] = dt_ref[:, lanes]
        da_ref[slot, dim:, :] = jnp.concatenate(pieces(-delta, 3) + [fill], axis=0)
        g_ref[slot] = nn(v_ref[...], da_ref[slot])
        return share

    share = grads(0)
    for r in range(nr):
        slot, lanes = r % 2, slice(r * rows, (r + 1) * rows)
        after = grads(r + 1) if r + 1 < nr else None
        for j in range(nk):
            span = slice(j * tok, (j + 1) * tok)
            p = p_ref[span, lanes].astype(F32)
            t_ref[slot, span, :] = (p * g_ref[slot, span, :]).astype(BF16)
        value_part = nn(p_ref[:, lanes], (dt_ref[:, lanes].astype(F32) * share).astype(BF16).T)
        key_part = nn(t_ref[slot], (qt_ref[:, lanes].astype(F32) * share).astype(BF16).T)
        if r == 0:
            acc_ref[:, :dim] = key_part
            acc_ref[:, dim:] = value_part
        else:
            acc_ref[:, :dim] += key_part
            acc_ref[:, dim:] += value_part
        query_part = tn(k_ref[...], t_ref[slot]) * (share * scale)
        for h in range(width // dim):
            piece = query_part[:, h * tok : (h + 1) * tok].astype(outs[r].dtype).T
            outs[r][:, h * dim : (h + 1) * dim] = piece
        share = after
    half = nk // 2
    for j in range(nk):
        ref = keep_ref if j < half else send_ref
        span = slice(j % half * tok, (j % half + 1) * tok)
        cols = slice(j * tok, (j + 1) * tok)
        ref[span, :dim] = (acc_ref[cols, :dim] * scale).astype(ref.dtype)
        ref[span, dim:] = acc_ref[cols, dim:].astype(ref.dtype)


def attended_kernel(count, dim, *refs):
    stats, parts, out = refs[:count], refs[count : 2 * count], refs[2 * count]
    tok, width = out.shape
    shares, _ = joined(stats, 0)
    for h in range(width // dim):
        total = None
        across = [share[:, h * tok : (h + 1) * tok] for share in shares]
        across += [jnp.zeros_like(across[0])] * (-count % 8)
        columns = jnp.concatenate(across, axis=0).T
        for a in range(count):
            part = parts[a][:, h * dim : (h + 1) * dim].astype(F32) * columns[:, a : a + 1]
            total = part if total is None else total + part
        out[:, h * dim : (h + 1) * dim] = total


def call(kernel, outs, *args, scalars=0, spaces=VMEM, scratch=(), flops=0, room=None):
    nbytes = sum(a.size * a.dtype.itemsize for a in (*args, *outs))
    return pl.pallas_call(
        kernel,
        out_shape=outs,
        in_specs=[SMEM] * scalars + [spaces] * (len(args) - scalars),
        out_specs=[VMEM] * len(outs),
        scratch_shapes=list(scratch),
        compiler_params=pltpu.CompilerParams(vmem_limit_bytes=room) if room else None,
        cost_estimate=pl.CostEstimate(flops=flops, bytes_accessed=nbytes, transcendentals=0),
    )(*args)


def per_device(queries, keys, values, upstream, block_order):
    tok, width = queries.shape
    dim = keys.shape[1]
    heads = width // dim
    rows = tok * heads
    nrow, ncol = lax.axis_size("qrow"), lax.axis_size("kcol")
    devices = nrow * ncol
    row_bits = [ncol << i for i in range(1, nrow.bit_length() - 1)] + [1]
    far_bits = [1 << i for i in range(1, ncol.bit_length() - 1)]
    pair = ncol
    row_masks = spread(row_bits)
    far_masks = spread(far_bits)
    key_masks = far_masks + [pair | mask for mask in far_masks]
    nr, nf, nk = len(row_masks), len(far_masks), len(key_masks)
    me = (lax.axis_index("qrow") * ncol + lax.axis_index("kcol")).astype(jnp.int32).reshape(1)

    def send(value, mask):
        return swap(value, mask, devices)

    def spray(values, masks):
        return [send(v, mask) for v, mask in zip(values, masks[1:])]

    def shape(dims, kind):
        return jax.ShapeDtypeStruct(dims, kind)

    given = (block_order, queries, upstream, keys, values)
    own_rows, own, bias = call(
        lambda *refs: pack_kernel(row_masks, key_masks, *refs),
        [
            shape((tok, 2 * width), BF16),
            shape((tok, 2 * dim), BF16),
            shape((nr, max(128, nk)), F32),
        ],
        me, *[pltpu.with_memory_space_constraint(a, pltpu.HBM) for a in given],
        scalars=1, spaces=pl.BlockSpec(memory_space=pltpu.HBM),
        scratch=[pltpu.SMEM(block_order.shape, jnp.int32), pltpu.SemaphoreType.DMA((5,))],
        room=4 << 20,
    )
    qd = [own_rows] + spray([own_rows] * (nr - 1), row_masks)
    far = [own] + spray([own] * (nf - 1), far_masks)
    kv = far + [send(part, pair) for part in far]

    score = pltpu.VMEM((2, nk * tok, rows), F32)
    narrow, wide = pltpu.VMEM((nk * tok, dim), BF16), pltpu.VMEM((nk * tok, 2 * dim), BF16)
    room = 4 * nk * tok * nr * rows
    work = 2 * rows * nr * tok * nk * dim
    stats, weights, flat_q, flat_d, *parts = call(
        lambda *refs: forward_kernel(nr, nk, *refs),
        [
            shape((4 * nr, rows), F32),
            shape((nk * tok, nr * rows), BF16),
            shape((dim, nr * rows), BF16),
            shape((dim, nr * rows), BF16),
            shape((tok, width), F32),
        ]
        + [shape((tok, width), BF16)] * (nr - 1),
        bias, *qd, *kv,
        scratch=[wide, narrow, score], flops=2 * work, room=room + (6 << 20),
    )
    all_stats = [stats] + spray([stats] * (nr - 1), row_masks)
    all_parts = parts[:1] + spray(parts[1:], row_masks)
    *row_parts, keep, give = call(
        lambda *refs: backward_kernel(nr, nk, *refs),
        [shape((tok, width), F32)]
        + [shape((tok, width), BF16)] * (nr - 1)
        + [shape((nf * tok, 2 * dim), F32), shape((nf * tok, 2 * dim), BF16)],
        weights, flat_q, flat_d, *all_stats, *kv,
        scratch=[
            narrow,
            wide,
            pltpu.VMEM((2, 2 * dim, rows), BF16),
            score,
            pltpu.VMEM((2, nk * tok, rows), BF16),
            pltpu.VMEM((nk * tok, 2 * dim), F32),
        ],
        flops=4 * work,
        room=room + (8 << 20),
    )
    got = send(give, pair)
    summed = keep + got.astype(F32)
    own_kv, *far_kv = [summed[i * tok : (i + 1) * tok] for i in range(nf)]
    far_kv = [part.astype(BF16) for part in far_kv]
    rows_in = spray(row_parts[1:], row_masks)
    far_in = spray(far_kv, far_masks)
    (attended,) = call(
        lambda *refs: attended_kernel(nr, dim, *refs),
        [shape((tok, width), F32)], *all_stats, *all_parts,
        room=8 * nr * tok * width + (4 << 20),
    )
    query_grad = row_parts[0] + sum(part.astype(F32) for part in rows_in)
    key_sum = own_kv + sum(part.astype(F32) for part in far_in)
    key_grad, value_grad = key_sum[:, :dim], key_sum[:, dim:]
    return attended, query_grad, key_grad, value_grad


def solution(mesh):
    spec = P(AXES, None)

    return jax.shard_map(
        per_device,
        mesh=mesh,
        in_specs=(spec,) * 4 + (P(),),
        out_specs=(spec,) * 4,
        check_vma=False,
    )
```

```python
import math

import jax
import jax.numpy as jnp
from jax import lax
from jax.experimental import pallas as pl
from jax.experimental.pallas import tpu as pltpu
from jax.sharding import PartitionSpec as P


AXES = ("qrow", "kcol")
F32, BF16 = jnp.float32, jnp.bfloat16
HIDDEN = 1e30
FLOOR = -1e29
LOG2E = math.log2(math.e)
VMEM = pl.BlockSpec(memory_space=pltpu.VMEM)
SMEM = pl.BlockSpec(memory_space=pltpu.SMEM)


def spread(bits):
    return [
        sum(bit for place, bit in enumerate(bits) if index >> place & 1)
        for index in range(1 << len(bits))
    ]


def swap(value, mask, devices):
    return lax.ppermute(value, AXES, [(i, i ^ mask) for i in range(devices)])


def nn(a, b):
    return lax.dot_general(a, b, (((1,), (0,)), ((), ())), preferred_element_type=F32)


def tn(a, b):
    return lax.dot_general(a, b, (((0,), (0,)), ((), ())), preferred_element_type=F32)


def by_head(ref, dim, start, width):
    return jnp.concatenate(
        [ref[:, at : at + dim].T for at in range(start, start + width, dim)], axis=1
    )


def pieces(value, count):
    parts = []
    for _ in range(count):
        part = value.astype(BF16)
        value = value - part.astype(F32)
        parts.append(part)
    return parts


def seen_in_block(tok, rows):
    key = lax.broadcasted_iota(jnp.int32, (tok, rows), 0)
    row = lax.broadcasted_iota(jnp.int32, (tok, rows), 1) % tok
    return key <= row


def pack_kernel(row_masks, key_masks, me_ref, table_ref, *refs):
    ins, (rows_ref, keys_ref, bias_ref, order_ref, sems) = refs[:4], refs[4:]
    width, dim = ins[0].shape[1], ins[2].shape[1]
    spots = [
        rows_ref.at[:, :width],
        rows_ref.at[:, width:],
        keys_ref.at[:, :dim],
        keys_ref.at[:, dim:],
    ]
    copies = [
        pltpu.make_async_copy(source, spot, sems.at[i])
        for i, (source, spot) in enumerate(zip((table_ref, *ins), (order_ref, *spots)))
    ]
    for copy in copies:
        copy.start()
    copies[0].wait()
    me = me_ref[0]
    lane = lax.broadcasted_iota(jnp.int32, (1, bias_ref.shape[1]), 1)
    for r, row_mask in enumerate(row_masks):
        row = jnp.zeros(lane.shape, F32)
        for j, key_mask in enumerate(key_masks):
            seen = order_ref[me ^ key_mask] <= order_ref[me ^ row_mask]
            row = jnp.where(lane == j, jnp.where(seen, jnp.float32(0.0), jnp.float32(HIDDEN)), row)
        bias_ref[r : r + 1, :] = row
    for copy in copies[1:]:
        copy.wait()


def forward_kernel(nr, nk, bias_ref, *refs):
    qds, kvs = refs[:nr], refs[nr : nr + nk]
    stats_ref, p_ref, qt_ref, dt_ref = refs[nr + nk : nr + nk + 4]
    outs, (kk_ref, v_ref, s_ref) = refs[nr + nk + 4 : -3], refs[-3:]
    tok, width = qds[0].shape[0], qds[0].shape[1] // 2
    dim = kvs[0].shape[1] // 2
    rows = tok * (width // dim)
    unit = dim**-0.5 * LOG2E
    for j, ref in enumerate(kvs):
        span = slice(j * tok, (j + 1) * tok)
        kk_ref[span, :dim] = ref[:, :dim]
        kk_ref[span, dim:] = ref[:, :dim]
        v_ref[span, :dim] = ref[:, dim:]
        v_ref[span, dim:] = jnp.ones((tok, dim), BF16)

    def score(r):
        q = by_head(qds[r], dim, 0, width)
        qt_ref[:, r * rows : (r + 1) * rows] = q
        scaled = jnp.concatenate(pieces(q.astype(F32) * unit, 2), axis=0)
        s_ref[r % 2] = nn(kk_ref[...], scaled)

    score(0)
    for r in range(nr):
        slot, lanes = r % 2, slice(r * rows, (r + 1) * rows)
        biases, top = [], None
        for j in range(nk):
            span = slice(j * tok, (j + 1) * tok)
            s = s_ref[slot, span, :]
            if r == 0 and j == 0:
                s = jnp.where(seen_in_block(tok, rows), s, -HIDDEN)
                s_ref[slot, span, :] = s
            bias = bias_ref[r : r + 1, j : j + 1]
            biases.append(bias)
            part = jnp.max(s, axis=0, keepdims=True) - bias
            top = part if top is None else jnp.maximum(top, part)
        top = jnp.maximum(top, FLOOR)
        if r + 1 < nr:
            score(r + 1)
        for j in range(nk):
            span = slice(j * tok, (j + 1) * tok)
            p = jnp.exp2(s_ref[slot, span, :] - (top + biases[j]))
            p_ref[span, lanes] = p.astype(BF16)
        d = by_head(qds[r], dim, width, width)
        dt_ref[:, lanes] = d
        out = tn(v_ref[:, : dim + 16], p_ref[:, lanes])
        out, total = out[:dim], out[dim : dim + 1]
        for h in range(width // dim):
            piece = out[:, h * tok : (h + 1) * tok].astype(outs[r].dtype).T
            outs[r][:, h * dim : (h + 1) * dim] = piece
        stats_ref[4 * r : 4 * r + 1, :] = top
        stats_ref[4 * r + 1 : 4 * r + 2, :] = total
        stats_ref[4 * r + 2 : 4 * r + 3, :] = jnp.sum(out * d.astype(F32), axis=0, keepdims=True)
        stats_ref[4 * r + 3 : 4 * r + 4, :] = jnp.zeros_like(top)


def joined(stats, r):
    held = [ref[4 * (r ^ a) : 4 * (r ^ a) + 3, :] for a, ref in enumerate(stats)]
    best = held[0][0:1]
    for part in held[1:]:
        best = jnp.maximum(best, part[0:1])
    shares = [jnp.exp2(part[0:1] - best) for part in held]
    total = sum(share * part[1:2] for share, part in zip(shares, held))
    prods = sum(share * part[2:3] for share, part in zip(shares, held))
    inverse = 1.0 / total
    return [share * inverse for share in shares], prods * inverse


def backward_kernel(nr, nk, *refs):
    p_ref, qt_ref, dt_ref = refs[:3]
    stats, kvs = refs[3 : nr + 3], refs[nr + 3 : nr + nk + 3]
    outs = refs[nr + nk + 3 : 2 * nr + nk + 3]
    keep_ref, send_ref, k_ref, v_ref, da_ref, g_ref, t_ref, acc_ref = refs[2 * nr + nk + 3 :]
    tok, dim = kvs[0].shape[0], kvs[0].shape[1] // 2
    rows = p_ref.shape[1] // nr
    width = rows // tok * dim
    scale = dim**-0.5
    lane = lax.broadcasted_iota(jnp.int32, (tok, dim), 1)
    ones = jnp.where(lane < 3, jnp.float32(1.0), jnp.float32(0.0)).astype(BF16)
    for j, ref in enumerate(kvs):
        span = slice(j * tok, (j + 1) * tok)
        k_ref[span, :] = ref[:, :dim]
        v_ref[span, :dim] = ref[:, dim:]
        v_ref[span, dim:] = ones
    fill = jnp.zeros((dim - 3, rows), BF16)

    def grads(r):
        slot, lanes = r % 2, slice(r * rows, (r + 1) * rows)
        (share, *_), delta = joined(stats, r)
        da_ref[slot, :dim, :] = dt_ref[:, lanes]
        da_ref[slot, dim:, :] = jnp.concatenate(pieces(-delta, 3) + [fill], axis=0)
        g_ref[slot] = nn(v_ref[...], da_ref[slot])
        return share

    share = grads(0)
    for r in range(nr):
        slot, lanes = r % 2, slice(r * rows, (r + 1) * rows)
        after = grads(r + 1) if r + 1 < nr else None
        for j in range(nk):
            span = slice(j * tok, (j + 1) * tok)
            p = p_ref[span, lanes].astype(F32)
            t_ref[slot, span, :] = (p * g_ref[slot, span, :]).astype(BF16)
        value_part = nn(p_ref[:, lanes], (dt_ref[:, lanes].astype(F32) * share).astype(BF16).T)
        key_part = nn(t_ref[slot], (qt_ref[:, lanes].astype(F32) * share).astype(BF16).T)
        if r == 0:
            acc_ref[:, :dim] = key_part
            acc_ref[:, dim:] = value_part
        else:
            acc_ref[:, :dim] += key_part
            acc_ref[:, dim:] += value_part
        query_part = tn(k_ref[...], t_ref[slot]) * (share * scale)
        for h in range(width // dim):
            piece = query_part[:, h * tok : (h + 1) * tok].astype(outs[r].dtype).T
            outs[r][:, h * dim : (h + 1) * dim] = piece
        share = after
    half = nk // 2
    for j in range(nk):
        ref = keep_ref if j < half else send_ref
        span = slice(j % half * tok, (j % half + 1) * tok)
        cols = slice(j * tok, (j + 1) * tok)
        ref[span, :dim] = (acc_ref[cols, :dim] * scale).astype(ref.dtype)
        ref[span, dim:] = acc_ref[cols, dim:].astype(ref.dtype)


def attended_kernel(count, dim, *refs):
    stats, parts, out = refs[:count], refs[count : 2 * count], refs[2 * count]
    tok, width = out.shape
    shares, _ = joined(stats, 0)
    for h in range(width // dim):
        total = None
        across = [share[:, h * tok : (h + 1) * tok] for share in shares]
        across += [jnp.zeros_like(across[0])] * (-count % 8)
        columns = jnp.concatenate(across, axis=0).T
        for a in range(count):
            part = parts[a][:, h * dim : (h + 1) * dim].astype(F32) * columns[:, a : a + 1]
            total = part if total is None else total + part
        out[:, h * dim : (h + 1) * dim] = total


def call(kernel, outs, *args, scalars=0, spaces=VMEM, scratch=(), flops=0, room=None):
    nbytes = sum(a.size * a.dtype.itemsize for a in (*args, *outs))
    return pl.pallas_call(
        kernel,
        out_shape=outs,
        in_specs=[SMEM] * scalars + [spaces] * (len(args) - scalars),
        out_specs=[VMEM] * len(outs),
        scratch_shapes=list(scratch),
        compiler_params=pltpu.CompilerParams(vmem_limit_bytes=room) if room else None,
        cost_estimate=pl.CostEstimate(flops=flops, bytes_accessed=nbytes, transcendentals=0),
    )(*args)


def per_device(queries, keys, values, upstream, block_order):
    tok, width = queries.shape
    dim = keys.shape[1]
    heads = width // dim
    rows = tok * heads
    nrow, ncol = lax.axis_size("qrow"), lax.axis_size("kcol")
    devices = nrow * ncol
    row_bits = [ncol << i for i in range(1, nrow.bit_length() - 1)] + [1]
    far_bits = [1 << i for i in range(1, ncol.bit_length() - 1)]
    pair = ncol
    row_masks = spread(row_bits)
    far_masks = spread(far_bits)
    key_masks = far_masks + [pair | mask for mask in far_masks]
    nr, nf, nk = len(row_masks), len(far_masks), len(key_masks)
    me = (lax.axis_index("qrow") * ncol + lax.axis_index("kcol")).astype(jnp.int32).reshape(1)

    def send(value, mask):
        return swap(value, mask, devices)

    def spray(values, masks):
        return [send(v, mask) for v, mask in zip(values, masks[1:])]

    def shape(dims, kind):
        return jax.ShapeDtypeStruct(dims, kind)

    given = (block_order, queries, upstream, keys, values)
    own_rows, own, bias = call(
        lambda *refs: pack_kernel(row_masks, key_masks, *refs),
        [
            shape((tok, 2 * width), BF16),
            shape((tok, 2 * dim), BF16),
            shape((nr, max(128, nk)), F32),
        ],
        me, *[pltpu.with_memory_space_constraint(a, pltpu.HBM) for a in given],
        scalars=1, spaces=pl.BlockSpec(memory_space=pltpu.HBM),
        scratch=[pltpu.SMEM(block_order.shape, jnp.int32), pltpu.SemaphoreType.DMA((5,))],
        room=4 << 20,
    )
    qd = [own_rows] + spray([own_rows] * (nr - 1), row_masks)
    far = [own] + spray([own] * (nf - 1), far_masks)
    kv = far + [send(part, pair) for part in far]

    score = pltpu.VMEM((2, nk * tok, rows), F32)
    narrow, wide = pltpu.VMEM((nk * tok, dim), BF16), pltpu.VMEM((nk * tok, 2 * dim), BF16)
    room = 4 * nk * tok * nr * rows
    work = 2 * rows * nr * tok * nk * dim
    stats, weights, flat_q, flat_d, *parts = call(
        lambda *refs: forward_kernel(nr, nk, *refs),
        [
            shape((4 * nr, rows), F32),
            shape((nk * tok, nr * rows), BF16),
            shape((dim, nr * rows), BF16),
            shape((dim, nr * rows), BF16),
            shape((tok, width), F32),
        ]
        + [shape((tok, width), BF16)] * (nr - 1),
        bias, *qd, *kv,
        scratch=[wide, wide, score], flops=2 * work, room=room + (6 << 20),
    )
    all_stats = [stats] + spray([stats] * (nr - 1), row_masks)
    all_parts = parts[:1] + spray(parts[1:], row_masks)
    *row_parts, keep, give = call(
        lambda *refs: backward_kernel(nr, nk, *refs),
        [shape((tok, width), F32)]
        + [shape((tok, width), BF16)] * (nr - 1)
        + [shape((nf * tok, 2 * dim), F32), shape((nf * tok, 2 * dim), BF16)],
        weights, flat_q, flat_d, *all_stats, *kv,
        scratch=[
            narrow,
            wide,
            pltpu.VMEM((2, 2 * dim, rows), BF16),
            score,
            pltpu.VMEM((2, nk * tok, rows), BF16),
            pltpu.VMEM((nk * tok, 2 * dim), F32),
        ],
        flops=4 * work,
        room=room + (8 << 20),
    )
    got = send(give, pair)
    summed = keep + got.astype(F32)
    own_kv, *far_kv = [summed[i * tok : (i + 1) * tok] for i in range(nf)]
    far_kv = [part.astype(BF16) for part in far_kv]
    rows_in = spray(row_parts[1:], row_masks)
    far_in = spray(far_kv, far_masks)
    (attended,) = call(
        lambda *refs: attended_kernel(nr, dim, *refs),
        [shape((tok, width), F32)], *all_stats, *all_parts,
        room=8 * nr * tok * width + (4 << 20),
    )
    query_grad = row_parts[0] + sum(part.astype(F32) for part in rows_in)
    key_sum = own_kv + sum(part.astype(F32) for part in far_in)
    key_grad, value_grad = key_sum[:, :dim], key_sum[:, dim:]
    return attended, query_grad, key_grad, value_grad


def solution(mesh):
    spec = P(AXES, None)

    return jax.shard_map(
        per_device,
        mesh=mesh,
        in_specs=(spec,) * 4 + (P(),),
        out_specs=(spec,) * 4,
        check_vma=False,
    )
```
